32 devices in a mesh: dp: 4 (over z), section: 2 (over core), tensor: 4 (over y, x).
Axes of the slice: x: 2, y: 2, z: 4, core: 2. Of those that a mesh axis runs over, the one named last changes fastest.
Arguments:
- tokens: bfloat16 [1024, 8192], P('dp', 'tensor'), may hold values from -6 to 6
- dest_slot: int32 [1024], P('dp'), may hold values from 0 to 1023, as said below
- doc_reset: int32 [1024], P('dp'), may hold values 0 or 1
- norm_gain: float32 [2, 8192], P('section'), may hold values from 0.25 to 1.75
- w_in: bfloat16 [2, 8192, 5120], P('section', 'dp', 'tensor'), may hold values from -0.0625 to 0.0625
- w_step: bfloat16 [2, 8192, 32], P('section', None, 'tensor'), may hold values from -0.0625 to 0.0625
- step_bias: float32 [2, 32], P('section', 'tensor'), may hold values from -4 to -1.5
- a_log: float32 [2, 32], P('section', 'tensor'), may hold values from -2.5 to 1.5
- d_skip: float32 [2, 32], P('section', 'tensor'), may hold values from 0.3 to 2
- out_gain: float32 [2, 2048], P('section', 'tensor'), may hold values from 0.25 to 1.75
- w_out: bfloat16 [2, 2048, 8192], P('section', 'tensor'), may hold values from -0.125 to 0.125
Outputs:
- phase_out: bfloat16 [2, 1024, 8192], P('section', 'dp', 'tensor')
The draws below stay inside these ranges and needn't reach their ends.
Inputs may be any that keep to these rules, and one draw needn't show every extreme that they name: dest_slot is a permutation; the tokens of one group go in order to increasing groups, and each group receives rows in order of source group. One group sends at most 128 tokens to one group, and every group sends exactly 128 to some group.
All inputs are finite; a program needn't handle non-finite values. No bound on the sum of `doc_reset` on one device may be relied on, other than what follows from the above.
Results may differ from the reference program's by a relative error of at most 0.018.
Values may be sent and summed in bfloat16 or wider, within the bound.
A program may use at most 128 MiB of HBM per device.

```python
import jax
import jax.numpy as jnp
from jax import lax

D = 8192
HEAD_DIM = 64
STATE = 128
HEADS_DEV = 8
SPAN = 64
ROWS = 256
HEADS = 32
TOKENS = 1024
COLS = 5120
N_DP = 4
N_SECTION = 2
N_TENSOR = 4


def draw_dest_slot(key, part):
    share = ROWS // N_DP
    key_order = jax.random.fold_in(key, 7101)
    key_shift = jax.random.fold_in(key, 7203)
    scores = jax.random.randint(key_order, (N_DP,), 0, 1 << 20) * N_DP + jnp.arange(N_DP)
    sigma = jnp.argsort(scores).astype(jnp.int32)
    offset = jax.random.randint(key_shift, (), 1, N_DP)
    source = jnp.arange(N_DP)
    plus_to = sigma
    minus_to = sigma[(source + offset) % N_DP]
    target = jnp.arange(N_DP)[None, :]
    counts = share + share * (target == plus_to[:, None]).astype(jnp.int32) - share * (target == minus_to[:, None]).astype(jnp.int32)
    ends = jnp.cumsum(counts, axis=1)
    starts = ends - counts
    earlier = jnp.cumsum(counts, axis=0) - counts
    everyrow = jnp.arange(ROWS * N_DP)
    src_group = everyrow // ROWS
    within_src = everyrow % ROWS
    dst_group = jnp.sum((ends[src_group] <= within_src[:, None]).astype(jnp.int32), axis=1)
    within_dst = within_src - starts[src_group, dst_group]
    return (dst_group * ROWS + earlier[src_group, dst_group] + within_dst).astype(jnp.int32)


def set_ends(result, rng, smallest, top_value):
    dims = result.shape
    index_at = [jax.random.randint(jax.random.fold_in(rng, axis), (), 0, dims[axis]) for axis in range(len(dims))]
    result = result.at[tuple(index_at)].set(smallest)
    longest = dims.index(max(dims))
    index_at[longest] = (index_at[longest] + 1) % dims[longest]
    return result.at[tuple(index_at)].set(top_value)


def shard_levels(rng, shape, cuts, smallest, largest):
    level = 1.0
    for axis_at, blocks in cuts:
        heights = jax.random.uniform(jax.random.fold_in(jax.random.fold_in(rng, 6), axis_at), (blocks,), jnp.float32, smallest / len(cuts), largest / len(cuts))
        level = level * jnp.repeat(jnp.exp(heights), shape[axis_at] // blocks).reshape((-1,) + (1,) * (len(shape) - 1 - axis_at))
    return level


def bell_draw(rng, extent, deviation, reach, cuts=(), held_as=jnp.bfloat16):
    entries = jax.random.normal(rng, extent, jnp.float32) * deviation
    if len(cuts) > 0:
        entries = shard_levels(rng, extent, cuts, -0.22, 0.18) * entries
    return jnp.clip(entries, min=-reach, max=reach).astype(held_as)


def setup_inputs(seed: int = 0) -> dict:
    key_of = jax.random.split(jax.random.key(seed), 12)
    tokens = bell_draw(key_of[0], (TOKENS, D), 1.0, 6.0, ((0, 4), (1, 4)))
    dest_slot = draw_dest_slot(jax.random.fold_in(key_of[11], 71), 0)
    doc_reset = set_ends((jax.random.randint(key_of[2], (TOKENS,), 0, 48) < 1).astype(jnp.int32), jax.random.fold_in(key_of[2], 1), 0, 1)
    norm_gain = jnp.clip(1.0 + 0.15 * jax.random.normal(key_of[3], (N_SECTION, D), jnp.float32), 0.25, 1.75)
    w_in = bell_draw(key_of[4], (N_SECTION, D, COLS), D ** -0.5, 0.0625, ((0, 2), (1, 4), (2, 4)))
    w_step = bell_draw(key_of[5], (N_SECTION, D, HEADS), D ** -0.5, 0.0625, ((0, 2), (2, 4)))
    step_bias = jnp.clip(-4.0 + 2.5 * jax.random.uniform(key_of[6], (N_SECTION, HEADS), jnp.float32) ** shard_levels(key_of[6], (N_SECTION, HEADS), ((0, 2), (1, 4)), -0.2, 0.2), -4.0, -1.5)
    a_log = jnp.clip(-2.5 + 4.0 * jax.random.uniform(key_of[7], (N_SECTION, HEADS), jnp.float32) ** shard_levels(key_of[7], (N_SECTION, HEADS), ((0, 2), (1, 4)), -0.2, 0.2), -2.5, 1.5)
    d_skip = jnp.clip(0.3 + 1.7 * jax.random.uniform(key_of[8], (N_SECTION, HEADS), jnp.float32) ** shard_levels(key_of[8], (N_SECTION, HEADS), ((0, 2), (1, 4)), -0.2, 0.2), 0.3, 2.0)
    out_gain = jnp.clip(1.0 + 0.15 * jax.random.normal(key_of[9], (N_SECTION, HEADS * HEAD_DIM), jnp.float32), 0.25, 1.75)
    w_out = bell_draw(key_of[10], (N_SECTION, HEADS * HEAD_DIM, D), (HEADS * HEAD_DIM) ** -0.5, 0.125, ((0, 2), (1, 4)))
    return dict(tokens=tokens, dest_slot=dest_slot, doc_reset=doc_reset, norm_gain=norm_gain, w_in=w_in, w_step=w_step, step_bias=step_bias, a_log=a_log, d_skip=d_skip, out_gain=out_gain, w_out=w_out)


epsilon = 1e-05

def scan_block(inputs, writes, readout, step_size, log_decay, resets, state, skips):
    hp = lax.Precision.HIGHEST
    segment = jnp.cumsum(resets)
    cumulative = jnp.cumsum(log_decay, axis=0)
    positions = jnp.arange(resets.shape[0])
    in_segment = (segment[:, None] == segment[None, :]) & (positions[:, None] >= positions[None, :])
    gap = cumulative[:, None, :] - cumulative[None, :, :]
    decayed = jnp.where(in_segment[:, :, None], jnp.exp(jnp.where(in_segment[:, :, None], gap, 0.0)), 0.0)
    scores = jnp.einsum('thn,shn->tsh', readout, writes, precision=hp)
    weights = scores * decayed * step_size[None, :, :]
    output = jnp.einsum('tsh,shp->thp', weights, inputs, precision=hp)
    carry_ok = (segment == 0).astype(inputs.dtype)
    carried = jnp.einsum('thn,hpn->thp', readout, state, precision=hp)
    output = output + carry_ok[:, None, None] * jnp.exp(cumulative)[:, :, None] * carried
    last_seg = segment[-1]
    tail = (segment == last_seg).astype(inputs.dtype)[:, None] * jnp.exp(cumulative[-1][None, :] - cumulative) * step_size
    fresh = jnp.einsum('sh,shp,shn->hpn', tail, inputs, writes, precision=hp)
    kept = (last_seg == 0).astype(inputs.dtype) * jnp.exp(cumulative[-1])[:, None, None] * state
    output = output + skips[None, :, None] * inputs
    return (output, fresh + kept)

def scan_group(inputs, writes, readout, step_size, log_decay, resets, skips):
    blocks = ROWS // SPAN

    def split(arr):
        return arr.reshape((blocks, SPAN) + arr.shape[1:])

    def stepper(state, pieces):
        output, fresh = scan_block(*pieces, state, skips)
        return (fresh, output)
    start = jnp.zeros((HEADS, HEAD_DIM, STATE), inputs.dtype)
    _, outputs = lax.scan(stepper, start, (split(inputs), split(writes), split(readout), split(step_size), split(log_decay), split(resets)))
    return outputs.reshape((ROWS,) + outputs.shape[2:])

def reference(tokens, dest_slot, doc_reset, norm_gain, w_in, w_step, step_bias, a_log, d_skip, out_gain, w_out):
    per_block = 2 * HEADS_DEV * HEAD_DIM + 2 * STATE
    head_cols = HEADS_DEV * HEAD_DIM
    hidden = jnp.zeros_like(tokens).at[dest_slot].set(tokens)
    results = []
    for layer_idx in range(N_SECTION):
        widened = hidden.astype(jnp.float32)
        meansq = lax.optimization_barrier(jnp.mean(widened * widened, axis=-1, keepdims=True))
        normed_in = (widened * lax.rsqrt(meansq + epsilon) * norm_gain[layer_idx]).astype(jnp.bfloat16)
        proj = jnp.dot(normed_in, w_in[layer_idx], preferred_element_type=jnp.float32).astype(jnp.bfloat16)
        proj = proj.reshape(TOKENS, N_TENSOR, per_block)
        gate_proj = proj[:, :, :head_cols].astype(jnp.float32)
        inputs = proj[:, :, head_cols:2 * head_cols].astype(jnp.float32).reshape(TOKENS, HEADS, HEAD_DIM)
        writes = jnp.repeat(proj[:, :, 2 * head_cols:2 * head_cols + STATE].astype(jnp.float32), HEADS_DEV, axis=1)
        readout = jnp.repeat(proj[:, :, 2 * head_cols + STATE:].astype(jnp.float32), HEADS_DEV, axis=1)
        step_size = jax.nn.softplus(jnp.dot(normed_in, w_step[layer_idx], preferred_element_type=jnp.float32) + step_bias[layer_idx])
        log_decay = -jnp.exp(a_log[layer_idx]) * step_size

        def grouped(arr):
            return arr.reshape((N_DP, ROWS) + arr.shape[1:])
        mixed = jax.vmap(scan_group, in_axes=(0, 0, 0, 0, 0, 0, None))(grouped(inputs), grouped(writes), grouped(readout), grouped(step_size), grouped(log_decay), grouped(doc_reset), d_skip[layer_idx])
        mixed = mixed.reshape(TOKENS, N_TENSOR, head_cols)
        gated = mixed * jax.nn.silu(gate_proj)
        meansq_out = lax.optimization_barrier(jnp.mean(gated * gated, axis=-1, keepdims=True))
        normed = (gated * lax.rsqrt(meansq_out + epsilon) * out_gain[layer_idx].reshape(N_TENSOR, head_cols)).astype(jnp.bfloat16)
        summed = jnp.zeros((TOKENS, D), jnp.float32)
        for block_idx in range(N_TENSOR):
            rows_w = w_out[layer_idx][block_idx * head_cols:(block_idx + 1) * head_cols]
            partial_value = jnp.dot(normed[:, block_idx, :], rows_w, preferred_element_type=jnp.float32).astype(jnp.bfloat16)
            summed = summed + lax.optimization_barrier(partial_value).astype(jnp.float32)
        hidden = (widened + summed).astype(jnp.bfloat16)
        results.append(hidden)
    return jnp.stack(results)
```

```python
import jax
import jax.numpy as jnp
from jax import lax
from jax.experimental import pallas as pl
from jax.experimental.pallas import tpu as pltpu
from jax.sharding import PartitionSpec as P

HEAD_DIM = 64
STATE = 128
HEADS_DEV = 8
SPAN = 64
LANES = 128
TILE = 256
FEW = 16

epsilon = 1e-05
MESH = pl.DeviceIdType.MESH
F32, BF16 = jnp.float32, jnp.bfloat16


def rows(start, size):
    return pl.ds(pl.multiple_of(start, FEW), size)


def cols(start, size):
    return pl.ds(pl.multiple_of(start, LANES), size)


def nt_dot(a, b, precision=None):
    return lax.dot_general(
        a, b, (((1,), (1,)), ((), ())), precision=precision, preferred_element_type=F32
    )


def tn_dot(a, b):
    return lax.dot_general(a, b, (((0,), (0,)), ((), ())), preferred_element_type=F32)


def exact_dot(a, b):
    return jnp.dot(a, b, precision=lax.Precision.HIGHEST, preferred_element_type=F32)


def relay(
    tokens, dest_slot, resets, gain, w_in, w_step, step_bias, a_log, d_skip, out_gain, w_out
):
    groups, width, cores = lax.axis_size("dp"), lax.axis_size("tensor"), lax.axis_size("section")
    row_count, feat_local = tokens.shape
    feats = feat_local * width
    depth, n_cols = w_in.shape
    head_cols = HEADS_DEV * HEAD_DIM
    chunks = max(1, row_count // (FEW * width))
    chunk = row_count // chunks
    few = chunk // width
    quarter = row_count // width
    spans = chunk // SPAN
    total = groups * row_count
    flat = groups * chunk
    m_block = min(flat, TILE)

    def kernel(
        tok, slot_in, rst, gain, w_in_hbm, w_step, step_bias, a_log, d_skip, out_gain, w_out_hbm,
        out,
        w_in, w_out, T, X, sc, sl, oh, scol, U, XR, Y, YR, S, SR, PO, PR, hin, ho, un,
        state, consts, gated_s, normed_s,
        w_sem, l_sem, o_sem,
        a1_s, a1_r, sl_s, sl_r, a2_s, a2_r, c2_s, c2_r, a3_s, a3_r, c3_s, c3_r,
        y_s, y_r, p_s, p_r, k_s, k_r, o_s, o_r, h_s, h_r, d_s, d_r, z_s, z_r, g_s, g_r,
    ):
        group, lane, core = lax.axis_index("dp"), lax.axis_index("tensor"), lax.axis_index("section")
        first, last = core == 0, core == cores - 1

        def up(k):
            return lax.rem(group + k, groups)

        def down(k):
            return lax.rem(group + groups - k, groups)

        def right(k):
            return lax.rem(lane + k, width)

        def left(k):
            return lax.rem(lane + width - k, width)

        def send(src, dst, ss, rs, device):
            return pltpu.make_async_remote_copy(
                src_ref=src, dst_ref=dst, send_sem=ss, recv_sem=rs,
                device_id=device, device_id_type=MESH,
            )

        in_plane = range(1, width)
        in_line = range(1, groups)

        barrier = pltpu.get_barrier_semaphore()
        for k in in_plane:
            pl.semaphore_signal(barrier, inc=1, device_id={"tensor": right(k)}, device_id_type=MESH)
        for k in in_line:
            pl.semaphore_signal(barrier, inc=1, device_id={"dp": up(k)}, device_id_type=MESH)
        for k in range(1, cores):
            pl.semaphore_signal(
                barrier, inc=1, device_id={"section": lax.rem(core + k, cores)}, device_id_type=MESH
            )
        pl.semaphore_wait(barrier, width + groups + cores - 3)

        def a1(k):
            return send(
                tok.at[rows(right(k) * quarter, quarter), :],
                T.at[:, cols(lane * feat_local, feat_local)],
                a1_s.at[k - 1], a1_r.at[k - 1], {"tensor": right(k)},
            )

        def a1_in(k):
            return send(
                tok.at[rows(lane * quarter, quarter), :],
                T.at[:, cols(left(k) * feat_local, feat_local)],
                a1_s.at[k - 1], a1_r.at[k - 1], {"tensor": right(k)},
            )

        def slots(k, at):
            return send(slot_in, sl.at[at], sl_s.at[k - 1], sl_r.at[k - 1], {"dp": up(k)})

        def x_piece(s, q):
            return X.at[rows(s * row_count + q * quarter, quarter), :]

        def a2(k, at):
            return send(
                T.at[:, cols(up(k) * depth, depth)], x_piece(at, lane),
                a2_s.at[k - 1], a2_r.at[k - 1], {"dp": up(k)},
            )

        def c2(k, at):
            return send(
                sc.at[lane, group], sc.at[lane, at], c2_s.at[k - 1], c2_r.at[k - 1], {"dp": up(k)}
            )

        def a3(j, k, at):
            return send(
                x_piece(down(j), lane), x_piece(down(j), at),
                a3_s.at[j, k - 1], a3_r.at[j, k - 1], {"tensor": right(k)},
            )

        def c3(k, at):
            return send(sc.at[lane], sc.at[at], c3_s.at[k - 1], c3_r.at[k - 1], {"tensor": right(k)})

        def proj_out(c, k):
            return send(
                Y.at[c, rows(up(k) * chunk, chunk), :], YR.at[c, k - 1],
                y_s.at[c, k - 1], y_r.at[c, k - 1], {"dp": up(k)},
            )

        def side_out(c, k):
            return send(
                S.at[c, up(k)], SR.at[c, k - 1],
                p_s.at[c, k - 1], p_r.at[c, k - 1], {"dp": up(k)},
            )

        def kept_out(c, k, at):
            return send(
                XR.at[c, rows(up(k) * chunk + lane * few, few), :],
                hin.at[c, :, cols(at * depth, depth)],
                k_s.at[c, k - 1], k_r.at[c, k - 1], {"dp": up(k)},
            )

        def part_out(c, k):
            return send(
                PO.at[c, rows(right(k) * few, few), :], PR.at[c, k - 1],
                o_s.at[c, k - 1], o_r.at[c, k - 1], {"tensor": right(k)},
            )

        def hand_over(c):
            return send(
                ho.at[c], hin.at[c], h_s.at[c], h_r.at[c], {"section": lax.rem(core + 1, cores)}
            )

        def out_rows(c, q):
            return out.at[rows(c * chunk + q * few, few), :]

        def deliver(c, k, at):
            return send(
                ho.at[c, :, cols(right(k) * feat_local, feat_local)], out_rows(c, at),
                d_s.at[c, k - 1], d_r.at[c, k - 1], {"tensor": right(k)},
            )

        def keep(c):
            return pltpu.make_async_copy(
                ho.at[c, :, cols(lane * feat_local, feat_local)], out_rows(c, lane), o_sem.at[c]
            )

        def u_piece(c, s, q):
            return U.at[c, rows(s * chunk + q * few, few), :]

        def z_out(c, k, at):
            return send(
                un.at[c, :, cols(up(k) * depth, depth)], u_piece(c, at, lane),
                z_s.at[c, k - 1], z_r.at[c, k - 1], {"dp": up(k)},
            )

        def spread(c, j, k, at):
            return send(
                u_piece(c, down(j), lane), u_piece(c, down(j), at),
                g_s.at[c, j, k - 1], g_r.at[c, j, k - 1], {"tensor": right(k)},
            )

        own_t = pltpu.make_async_copy(
            tok.at[rows(lane * quarter, quarter), :],
            T.at[:, cols(lane * feat_local, feat_local)], l_sem.at[0],
        )
        own_x = pltpu.make_async_copy(
            T.at[:, cols(group * depth, depth)], x_piece(group, lane), l_sem.at[1]
        )
        load_in = pltpu.make_async_copy(w_in_hbm, w_in, w_sem.at[0])
        load_out = pltpu.make_async_copy(w_out_hbm, w_out, w_sem.at[1])

        @pl.when(first)
        def _():
            for k in in_plane:
                a1(k).start()
            own_t.start()
            for k in in_line:
                slots(k, group).start()

        load_in.start()
        load_out.start()

        row_at = lax.broadcasted_iota(jnp.int32, (LANES, LANES), 0)
        lane_at = lax.broadcasted_iota(jnp.int32, (LANES, LANES), 1)
        low = lane_at < SPAN
        inner = jnp.where(low, lane_at, lane_at - SPAN)
        consts[0] = ((row_at < SPAN) & (row_at <= inner)).astype(F32)
        consts[1] = ((row_at < SPAN) & (row_at == inner)).astype(F32)
        consts[2] = (lane_at <= row_at).astype(F32)
        consts[3] = (lane_at == row_at).astype(F32)
        state[...] = jnp.zeros_like(state)
        S[...] = jnp.zeros_like(S)

        @pl.when(first)
        def _():
            sl[group] = slot_in[...]
            own_t.wait()
            for k in in_plane:
                a1_in(k).wait_recv()
            for k in in_line:
                a2(k, group).start()
            own_x.start()
            wide = T[...].astype(F32)
            scale = lax.rsqrt(jnp.mean(wide * wide, axis=-1, keepdims=True) + epsilon)
            own_x.wait()
            for k in in_plane:
                a3(0, k, lane).start()
            spot = lax.rem(lane * quarter, LANES)
            i_at = lax.broadcasted_iota(jnp.int32, (quarter, LANES), 0)
            l_at = lax.broadcasted_iota(jnp.int32, (quarter, LANES), 1)
            line = jnp.sum(jnp.where(l_at == i_at + spot, scale, 0.0), axis=0, keepdims=True)
            sc[lane, group] = jnp.broadcast_to(line, (8, LANES))
            for k in in_line:
                c2(k, group).start()
            for j in in_line:
                a2(j, down(j)).wait_recv()
                for k in in_plane:
                    a3(j, k, lane).start()
            for j in in_line:
                c2(j, down(j)).wait_recv()
            for k in in_plane:
                c3(k, lane).start()
            for j in in_line:
                slots(j, down(j)).wait_recv()
            for k in in_plane:
                c3(k, left(k)).wait_recv()
                for j in range(groups):
                    a3(j, k, left(k)).wait_recv()

        load_in.wait()
        load_out.wait()

        def permute(c):
            for g in range(groups):
                wanted = (
                    g * row_count + c * chunk
                    + lax.broadcasted_iota(jnp.int32, (chunk, LANES), 0)
                )
                found = jnp.zeros((chunk, LANES), F32)
                for tile in range(total // LANES):
                    s, at = tile * LANES // row_count, tile * LANES % row_count
                    mask = sl[s, at // LANES : at // LANES + 1, :] == wanted
                    oh[g * chunk : (g + 1) * chunk, tile * LANES : (tile + 1) * LANES] = jnp.where(
                        mask, 1.0, 0.0
                    ).astype(BF16)
                    line = sc[at // quarter, s, 0:1, :]
                    for q in range(1, LANES // quarter):
                        line = line + sc[at // quarter + q, s, 0:1, :]
                    found = found + jnp.where(mask, line, 0.0)
                scol[g * chunk : (g + 1) * chunk, :] = jnp.broadcast_to(
                    jnp.sum(found, axis=1, keepdims=True), (chunk, LANES)
                )

            @pl.loop(0, flat // m_block)
            def _(m):
                here = rows(m * m_block, m_block)

                @pl.loop(0, depth // TILE)
                def _(n):
                    there = cols(n * TILE, TILE)
                    x = jnp.dot(oh[here, :], X[:, there], preferred_element_type=F32)
                    XR[c, here, there] = x.astype(BF16)
                    u = x * scol[here, 0:1] * gain[:, cols(group * depth + n * TILE, TILE)]
                    U[c, here, there] = u.astype(BF16)

            hin[c, :, cols(group * depth, depth)] = XR[c, rows(group * chunk + lane * few, few), :]
            for k in in_line:
                kept_out(c, k, group).start()

        def project(c):
            @pl.loop(0, flat // m_block)
            def _(m):
                here = rows(m * m_block, m_block)

                @pl.loop(0, n_cols // TILE)
                def _(n):
                    there = cols(n * TILE, TILE)
                    Y[c, here, there] = jnp.dot(
                        U[c, here, :], w_in[:, there], preferred_element_type=F32
                    ).astype(BF16)

            for g in range(groups):
                for b in range(spans):
                    at = g * chunk + b * SPAN
                    S[c, g, b, :, 0:SPAN] = nt_dot(w_step[...], U[c, at : at + SPAN, :])
            for k in in_line:
                side_out(c, k).start()
                proj_out(c, k).start()

        def scan_span(c, b):
            at = b * SPAN
            proj = Y[c, rows(group * chunk + at, SPAN), :].astype(F32)
            pre = S[c, group, b]
            for k in in_line:
                proj = proj + YR[c, k - 1, at : at + SPAN, :].astype(F32)
                pre = pre + SR[c, k - 1, b]
            proj = proj.astype(BF16)
            step = pre + step_bias[...]
            step = jnp.maximum(step, 0.0) + jnp.log1p(jnp.exp(-jnp.abs(step)))
            decay = -jnp.exp(a_log[...]) * step
            reset = rst[c * spans + b]
            to_rows, dup = consts[0], consts[1]
            to_cols, eye = consts[2][:SPAN], consts[3][:SPAN]
            hp = lax.Precision.HIGHEST
            cum_row, step_row, seg_row = (
                exact_dot(decay, to_rows), exact_dot(step, dup), exact_dot(reset, to_rows)
            )
            cum, step_col, seg = (
                nt_dot(to_cols, decay, hp), nt_dot(eye, step, hp), nt_dot(to_cols, reset, hp)
            )
            l_at = lax.broadcasted_iota(jnp.int32, (SPAN, LANES), 1)
            t_at = lax.broadcasted_iota(jnp.int32, (SPAN, LANES), 0)
            low = l_at < SPAN
            inside = (seg[:, 0:1] == seg_row[0:1, :]) & (t_at >= jnp.where(low, l_at, l_at - SPAN))
            top = cum[SPAN - 1 : SPAN, :]
            last_seg = seg[SPAN - 1 : SPAN, :]
            carry = jnp.where(seg == 0.0, jnp.exp(cum), 0.0)
            tail = jnp.where(seg == last_seg, jnp.exp(top - cum), 0.0) * step_col
            hold = jnp.where(last_seg == 0.0, jnp.exp(top), 0.0)
            writes = proj[:, 2 * head_cols : 2 * head_cols + STATE]
            reads = proj[:, 2 * head_cols + STATE :]
            scores = nt_dot(reads, jnp.concatenate([writes, writes], axis=0))
            squares = jnp.zeros((SPAN, LANES), F32)
            for j in range(head_cols // LANES):
                a, z = 2 * j, 2 * j + 1
                part = slice(j * LANES, (j + 1) * LANES)

                def pair_col(v):
                    return jnp.where(low, v[:, a : a + 1], v[:, z : z + 1])

                def pair_row(v):
                    return jnp.where(low[0:1], v[a : a + 1, :], v[z : z + 1, :])

                x = proj[:, head_cols + j * LANES : head_cols + (j + 1) * LANES].astype(F32)
                gap = jnp.where(inside, pair_col(cum) - pair_row(cum_row), 0.0)
                weights = jnp.where(inside, jnp.exp(gap), 0.0) * scores * pair_row(step_row)
                both = jnp.concatenate(
                    [jnp.where(low, x, 0.0), jnp.where(low, 0.0, x)], axis=0
                ).astype(BF16)
                y = jnp.dot(weights.astype(BF16), both, preferred_element_type=F32)
                held = state[:, part]
                y = y + pair_col(carry) * jnp.dot(
                    reads, held.astype(BF16), preferred_element_type=F32
                )
                y = y + d_skip[:, part] * x
                fresh = tn_dot(writes, (pair_col(tail) * x).astype(BF16))
                keep_by = jnp.where(low[0:1], hold[:, a : a + 1], hold[:, z : z + 1])
                state[:, part] = fresh + keep_by * held
                gate = proj[:, part].astype(F32)
                gated = y * (gate * lax.logistic(gate))
                squares = squares + gated * gated
                gated_s[:, part] = gated
            mean = jnp.sum(squares, axis=1, keepdims=True) / head_cols
            normed = gated_s[...] * lax.rsqrt(mean + epsilon) * out_gain[...]
            normed_s[at : at + SPAN, :] = normed.astype(BF16)

        def mix(c):
            for k in in_line:
                side_out(c, k).wait_recv()
                proj_out(c, k).wait_recv()
            for b in range(spans):
                scan_span(c, b)

            @pl.loop(0, feats // TILE)
            def _(n):
                there = cols(n * TILE, TILE)
                PO[c, :, there] = jnp.dot(
                    normed_s[...], w_out[:, there], preferred_element_type=F32
                ).astype(BF16)

            for k in in_plane:
                part_out(c, k).start()

        def finish(c):
            for k in in_plane:
                part_out(c, k).wait_recv()

            @pl.when(first)
            def _():
                for k in in_line:
                    kept_out(c, k, down(k)).wait_recv()

            @pl.loop(0, feats // (4 * TILE))
            def _(n):
                there = cols(n * 4 * TILE, 4 * TILE)
                added = PO[c, rows(lane * few, few), there].astype(F32)
                for k in in_plane:
                    added = added + PR[c, k - 1, :, there].astype(F32)
                ho[c, :, there] = (hin[c, :, there].astype(F32) + added).astype(BF16)

            @pl.when(jnp.logical_not(last))
            def _():
                hand_over(c).start()

            for k in in_plane:
                deliver(c, k, lane).start()
            keep(c).start()

        def normalise(c):
            hand_over(c).wait_recv()
            wide = hin[c].astype(F32)
            scale = lax.rsqrt(jnp.mean(wide * wide, axis=-1, keepdims=True) + epsilon)
            un[c] = (wide * scale * gain[...]).astype(BF16)
            for k in in_line:
                z_out(c, k, group).start()
            U[c, rows(group * chunk + lane * few, few), :] = un[c, :, cols(group * depth, depth)]
            for k in in_plane:
                spread(c, 0, k, lane).start()

        def forward(c):
            for j in in_line:
                z_out(c, j, down(j)).wait_recv()
                for k in in_plane:
                    spread(c, j, k, lane).start()

        def gathered(c):
            for k in in_plane:
                for j in range(groups):
                    spread(c, j, k, left(k)).wait_recv()

        mix_lag = jnp.where(first, 2, 1)
        end_lag = jnp.where(first, 3, 1)

        def turn(i, _):
            fresh = i < chunks

            @pl.when(fresh & jnp.logical_not(first))
            def _():
                normalise(i)

            m = i - mix_lag

            @pl.when((m >= 0) & (m < chunks))
            def _():
                mix(m)

            @pl.when(fresh & jnp.logical_not(first))
            def _():
                forward(i)

            e = i - end_lag

            @pl.when((e >= 0) & (e < chunks))
            def _():
                finish(e)

            @pl.when(fresh & first)
            def _():
                permute(i)

            @pl.when(fresh & jnp.logical_not(first))
            def _():
                gathered(i)

            @pl.when(fresh)
            def _():
                project(i)

            return 0

        lax.fori_loop(0, chunks + 3, turn, 0)

        def settle(c, _):
            keep(c).wait()
            for k in in_plane:
                deliver(c, k, left(k)).wait_recv()
                deliver(c, k, lane).wait_send()
                part_out(c, k).wait_send()
            for k in in_line:
                side_out(c, k).wait_send()
                proj_out(c, k).wait_send()

            @pl.when(first)
            def _():
                for k in in_line:
                    kept_out(c, k, group).wait_send()

            @pl.when(jnp.logical_not(first))
            def _():
                for k in in_line:
                    z_out(c, k, group).wait_send()
                for k in in_plane:
                    for j in range(groups):
                        spread(c, j, k, lane).wait_send()

            @pl.when(jnp.logical_not(last))
            def _():
                hand_over(c).wait_send()

            return 0

        lax.fori_loop(0, chunks, settle, 0)

        @pl.when(first)
        def _():
            for k in in_line:
                slots(k, group).wait_send()
                a2(k, group).wait_send()
                c2(k, group).wait_send()
            for k in in_plane:
                a1(k).wait_send()
                c3(k, lane).wait_send()
                for j in range(groups):
                    a3(j, k, lane).wait_send()

    vmem, dma = pltpu.VMEM, pltpu.SemaphoreType.DMA
    near, line = (width - 1,), (groups - 1,)
    scratch = [
        vmem((depth, n_cols), BF16),
        vmem((head_cols, feats), BF16),
        vmem((quarter, feats), BF16),
        vmem((total, depth), BF16),
        vmem((width, groups, 8, LANES), F32),
        vmem((groups, row_count // LANES, LANES), jnp.int32),
        vmem((flat, total), BF16),
        vmem((flat, LANES), F32),
        vmem((chunks, flat, depth), BF16),
        vmem((chunks, flat, depth), BF16),
        vmem((chunks, flat, n_cols), BF16),
        vmem((chunks, groups - 1, chunk, n_cols), BF16),
        vmem((chunks, groups, spans, 8, LANES), F32),
        vmem((chunks, groups - 1, spans, 8, LANES), F32),
        vmem((chunks, chunk, feats), BF16),
        vmem((chunks, width - 1, few, feats), BF16),
        vmem((chunks, few, feats), BF16),
        vmem((chunks, few, feats), BF16),
        vmem((chunks, few, feats), BF16),
        vmem((STATE, head_cols), F32),
        vmem((4, LANES, LANES), F32),
        vmem((SPAN, head_cols), F32),
        vmem((chunk, head_cols), BF16),
        dma((2,)), dma((2,)), dma((chunks,)),
    ]
    for shape in [
        near, line, line, line, (groups,) + near, near,
        (chunks,) + line, (chunks,) + line, (chunks,) + line, (chunks,) + near,
        (chunks,), (chunks,) + near, (chunks,) + line, (chunks, groups) + near,
    ]:
        scratch += [dma(shape), dma(shape)]
    anywhere = pl.BlockSpec(memory_space=pl.ANY)
    held = pl.BlockSpec(memory_space=pltpu.VMEM)
    return pl.pallas_call(
        kernel,
        out_shape=jax.ShapeDtypeStruct((row_count, feat_local), BF16),
        in_specs=[
            anywhere, held, held, held, anywhere, held, held, held, held, held, anywhere
        ],
        out_specs=anywhere,
        scratch_shapes=scratch,
        compiler_params=pltpu.CompilerParams(
            collective_id=0, has_side_effects=True, vmem_limit_bytes=63 * 1024 * 1024
        ),
    )(tokens, dest_slot, resets, gain, w_in, w_step, step_bias, a_log, d_skip, out_gain, w_out)


def per_device(
    tokens, dest_slot, doc_reset, norm_gain, w_in, w_step, step_bias, a_log, d_skip, out_gain, w_out
):
    group = lax.axis_index("dp")
    row_count = tokens.shape[0]
    depth = w_in.shape[1]
    own_step = lax.dynamic_slice_in_dim(w_step[0], group * depth, depth, axis=0).T
    resets = doc_reset.astype(F32).reshape(-1, 1, SPAN)
    resets = jnp.broadcast_to(jnp.pad(resets, ((0, 0), (0, 0), (0, LANES - SPAN))),
                              (row_count // SPAN, 8, LANES))
    out = relay(
        tokens,
        dest_slot.reshape(-1, LANES),
        resets,
        norm_gain,
        w_in[0],
        own_step,
        step_bias.reshape(-1, 1),
        a_log.reshape(-1, 1),
        jnp.repeat(d_skip, HEAD_DIM, axis=1),
        out_gain,
        w_out[0],
    )
    return out[None]


def solution(mesh):
    placed = (
        P("dp", "tensor"),
        P("dp"),
        P("dp"),
        P("section", None),
        P("section", "dp", "tensor"),
        P("section", None, "tensor"),
        P("section", "tensor"),
        P("section", "tensor"),
        P("section", "tensor"),
        P("section", "tensor"),
        P("section", "tensor", None),
    )
    return jax.shard_map(
        per_device,
        mesh=mesh,
        in_specs=placed,
        out_specs=P("section", "dp", "tensor"),
        check_vma=False,
    )
```

```python
import jax
import jax.numpy as jnp
from jax import lax
from jax.experimental import pallas as pl
from jax.experimental.pallas import tpu as pltpu
from jax.sharding import PartitionSpec as P

HEAD_DIM = 64
STATE = 128
HEADS_DEV = 8
SPAN = 64
LANES = 128
TILE = 256
WIDE = 1024
FEW = 16

epsilon = 1e-05
MESH = pl.DeviceIdType.MESH
F32, BF16 = jnp.float32, jnp.bfloat16


def rows(start, size):
    return pl.ds(pl.multiple_of(start, FEW), size)


def cols(start, size):
    return pl.ds(pl.multiple_of(start, LANES), size)


def nt_dot(a, b, precision=None):
    return lax.dot_general(
        a, b, (((1,), (1,)), ((), ())), precision=precision, preferred_element_type=F32
    )


def tn_dot(a, b):
    return lax.dot_general(a, b, (((0,), (0,)), ((), ())), preferred_element_type=F32)


def exact_dot(a, b):
    return jnp.dot(a, b, precision=lax.Precision.HIGHEST, preferred_element_type=F32)


def relay(
    tokens, dest_slot, resets, gain, w_in, w_step, step_bias, a_log, d_skip, out_gain, w_out
):
    groups, width, cores = lax.axis_size("dp"), lax.axis_size("tensor"), lax.axis_size("section")
    row_count, feat_local = tokens.shape
    feats = feat_local * width
    depth, n_cols = w_in.shape
    head_cols = HEADS_DEV * HEAD_DIM
    chunks = max(1, row_count // (FEW * width))
    chunk = row_count // chunks
    few = chunk // width
    quarter = row_count // width
    spans = chunk // SPAN
    total = groups * row_count
    flat = groups * chunk
    m_block = min(flat, TILE)

    def kernel(
        tok, slot_in, rst, gain, w_in_hbm, w_step, step_bias, a_log, d_skip, out_gain, w_out_hbm,
        out,
        w_in, w_out, T, X, sc, sl, oh, scol, U, XR, Y, YR, S, SR, PO, PR, hin, ho, un,
        state, consts, gated_s, normed_s,
        w_sem, l_sem, o_sem,
        a1_s, a1_r, sl_s, sl_r, a2_s, a2_r, c2_s, c2_r, a3_s, a3_r, c3_s, c3_r,
        y_s, y_r, p_s, p_r, k_s, k_r, o_s, o_r, h_s, h_r, d_s, d_r, z_s, z_r, g_s, g_r,
    ):
        group, lane, core = lax.axis_index("dp"), lax.axis_index("tensor"), lax.axis_index("section")
        first, last = core == 0, core == cores - 1

        def up(k):
            return lax.rem(group + k, groups)

        def down(k):
            return lax.rem(group + groups - k, groups)

        def right(k):
            return lax.rem(lane + k, width)

        def left(k):
            return lax.rem(lane + width - k, width)

        def send(src, dst, ss, rs, device):
            return pltpu.make_async_remote_copy(
                src_ref=src, dst_ref=dst, send_sem=ss, recv_sem=rs,
                device_id=device, device_id_type=MESH,
            )

        in_plane = range(1, width)
        in_line = range(1, groups)

        barrier = pltpu.get_barrier_semaphore()
        for k in in_plane:
            pl.semaphore_signal(barrier, inc=1, device_id={"tensor": right(k)}, device_id_type=MESH)
        for k in in_line:
            pl.semaphore_signal(barrier, inc=1, device_id={"dp": up(k)}, device_id_type=MESH)
        for k in range(1, cores):
            pl.semaphore_signal(
                barrier, inc=1, device_id={"section": lax.rem(core + k, cores)}, device_id_type=MESH
            )
        with jax.named_scope("barrier"):
            pl.semaphore_wait(barrier, width + groups + cores - 3)

        def a1(k):
            return send(
                tok.at[rows(right(k) * quarter, quarter), :],
                T.at[:, cols(lane * feat_local, feat_local)],
                a1_s.at[k - 1], a1_r.at[k - 1], {"tensor": right(k)},
            )

        def a1_in(k):
            return send(
                tok.at[rows(lane * quarter, quarter), :],
                T.at[:, cols(left(k) * feat_local, feat_local)],
                a1_s.at[k - 1], a1_r.at[k - 1], {"tensor": right(k)},
            )

        def slots(k, at):
            return send(slot_in, sl.at[at], sl_s.at[k - 1], sl_r.at[k - 1], {"dp": up(k)})

        def x_piece(s, q):
            return X.at[rows(s * row_count + q * quarter, quarter), :]

        def a2(k, at):
            return send(
                T.at[:, cols(up(k) * depth, depth)], x_piece(at, lane),
                a2_s.at[k - 1], a2_r.at[k - 1], {"dp": up(k)},
            )

        def c2(k, at):
            return send(
                sc.at[lane, group], sc.at[lane, at], c2_s.at[k - 1], c2_r.at[k - 1], {"dp": up(k)}
            )

        def a3(j, k, at):
            return send(
                x_piece(down(j), lane), x_piece(down(j), at),
                a3_s.at[j, k - 1], a3_r.at[j, k - 1], {"tensor": right(k)},
            )

        def c3(k, at):
            return send(sc.at[lane], sc.at[at], c3_s.at[k - 1], c3_r.at[k - 1], {"tensor": right(k)})

        def proj_out(c, k):
            return send(
                Y.at[c, rows(up(k) * chunk, chunk), :], YR.at[c, k - 1],
                y_s.at[c, k - 1], y_r.at[c, k - 1], {"dp": up(k)},
            )

        def side_out(c, k):
            return send(
                S.at[c, up(k)], SR.at[c, k - 1],
                p_s.at[c, k - 1], p_r.at[c, k - 1], {"dp": up(k)},
            )

        def kept_out(c, k, at):
            return send(
                XR.at[c, rows(up(k) * chunk + lane * few, few), :],
                hin.at[c, :, cols(at * depth, depth)],
                k_s.at[c, k - 1], k_r.at[c, k - 1], {"dp": up(k)},
            )

        def part_out(c, k):
            return send(
                PO.at[c, rows(right(k) * few, few), :], PR.at[c, k - 1],
                o_s.at[c, k - 1], o_r.at[c, k - 1], {"tensor": right(k)},
            )

        def hand_over(c):
            return send(
                ho.at[c], hin.at[c], h_s.at[c], h_r.at[c], {"section": lax.rem(core + 1, cores)}
            )

        def out_rows(c, q):
            return out.at[rows(c * chunk + q * few, few), :]

        def deliver(c, k, at):
            return send(
                ho.at[c, :, cols(right(k) * feat_local, feat_local)], out_rows(c, at),
                d_s.at[c, k - 1], d_r.at[c, k - 1], {"tensor": right(k)},
            )

        def keep(c):
            return pltpu.make_async_copy(
                ho.at[c, :, cols(lane * feat_local, feat_local)], out_rows(c, lane), o_sem.at[c]
            )

        def u_piece(c, s, q):
            return U.at[c, rows(s * chunk + q * few, few), :]

        def z_out(c, k, at):
            return send(
                un.at[c, :, cols(up(k) * depth, depth)], u_piece(c, at, lane),
                z_s.at[c, k - 1], z_r.at[c, k - 1], {"dp": up(k)},
            )

        def spread(c, j, k, at):
            return send(
                u_piece(c, down(j), lane), u_piece(c, down(j), at),
                g_s.at[c, j, k - 1], g_r.at[c, j, k - 1], {"tensor": right(k)},
            )

        own_t = pltpu.make_async_copy(
            tok.at[rows(lane * quarter, quarter), :],
            T.at[:, cols(lane * feat_local, feat_local)], l_sem.at[0],
        )
        own_x = pltpu.make_async_copy(
            T.at[:, cols(group * depth, depth)], x_piece(group, lane), l_sem.at[1]
        )
        load_in = pltpu.make_async_copy(w_in_hbm, w_in, w_sem.at[0])
        load_out = pltpu.make_async_copy(w_out_hbm, w_out, w_sem.at[1])

        @pl.when(first)
        def _():
            for k in in_plane:
                a1(k).start()
            own_t.start()
            for k in in_line:
                slots(k, group).start()

        load_in.start()
        load_out.start()

        row_at = lax.broadcasted_iota(jnp.int32, (LANES, LANES), 0)
        lane_at = lax.broadcasted_iota(jnp.int32, (LANES, LANES), 1)
        low = lane_at < SPAN
        inner = jnp.where(low, lane_at, lane_at - SPAN)
        consts[0] = ((row_at < SPAN) & (row_at <= inner)).astype(F32)
        consts[1] = ((row_at < SPAN) & (row_at == inner)).astype(F32)
        consts[2] = (lane_at <= row_at).astype(F32)
        consts[3] = (lane_at == row_at).astype(F32)
        state[...] = jnp.zeros_like(state)
        S[...] = jnp.zeros_like(S)

        @pl.when(first)
        def _():
            sl[group] = slot_in[...]
            with jax.named_scope("a1_wait"):
                own_t.wait()
                for k in in_plane:
                    a1_in(k).wait_recv()
            for k in in_line:
                a2(k, group).start()
            own_x.start()
            wide = T[...].astype(F32)
            scale = lax.rsqrt(jnp.mean(wide * wide, axis=-1, keepdims=True) + epsilon)
            own_x.wait()
            for k in in_plane:
                a3(0, k, lane).start()
            spot = lax.rem(lane * quarter, LANES)
            i_at = lax.broadcasted_iota(jnp.int32, (quarter, LANES), 0)
            l_at = lax.broadcasted_iota(jnp.int32, (quarter, LANES), 1)
            line = jnp.sum(jnp.where(l_at == i_at + spot, scale, 0.0), axis=0, keepdims=True)
            sc[lane, group] = jnp.broadcast_to(line, (8, LANES))
            for k in in_line:
                c2(k, group).start()
            with jax.named_scope("a2_wait"):
                for j in in_line:
                    a2(j, down(j)).wait_recv()
                    for k in in_plane:
                        a3(j, k, lane).start()
            with jax.named_scope("c2_wait"):
                for j in in_line:
                    c2(j, down(j)).wait_recv()
            for k in in_plane:
                c3(k, lane).start()
            for j in in_line:
                slots(j, down(j)).wait_recv()
            with jax.named_scope("a3_wait"):
                for k in in_plane:
                    c3(k, left(k)).wait_recv()
                    for j in range(groups):
                        a3(j, k, left(k)).wait_recv()

        with jax.named_scope("load_wait"):
            load_in.wait()
            load_out.wait()

        def permute(c):
            for g in range(groups):
                wanted = (
                    g * row_count + c * chunk
                    + lax.broadcasted_iota(jnp.int32, (chunk, LANES), 0)
                )
                found = jnp.zeros((chunk, LANES), F32)
                for tile in range(total // LANES):
                    s, at = tile * LANES // row_count, tile * LANES % row_count
                    mask = sl[s, at // LANES : at // LANES + 1, :] == wanted
                    oh[g * chunk : (g + 1) * chunk, tile * LANES : (tile + 1) * LANES] = jnp.where(
                        mask, 1.0, 0.0
                    ).astype(BF16)
                    line = sc[at // quarter, s, 0:1, :]
                    for q in range(1, LANES // quarter):
                        line = line + sc[at // quarter + q, s, 0:1, :]
                    found = found + jnp.where(mask, line, 0.0)
                scol[g * chunk : (g + 1) * chunk, :] = jnp.broadcast_to(
                    jnp.sum(found, axis=1, keepdims=True), (chunk, LANES)
                )

            @pl.loop(0, flat // m_block)
            def _(m):
                here = rows(m * m_block, m_block)

                @pl.loop(0, depth // TILE)
                def _(n):
                    there = cols(n * TILE, TILE)
                    x = jnp.dot(oh[here, :], X[:, there], preferred_element_type=F32)
                    XR[c, here, there] = x.astype(BF16)
                    u = x * scol[here, 0:1] * gain[:, cols(group * depth + n * TILE, TILE)]
                    U[c, here, there] = u.astype(BF16)

            hin[c, :, cols(group * depth, depth)] = XR[c, rows(group * chunk + lane * few, few), :]
            for k in in_line:
                kept_out(c, k, group).start()

        def project(c):
            @pl.loop(0, flat // m_block)
            def _(m):
                here = rows(m * m_block, m_block)

                @pl.loop(0, n_cols // TILE)
                def _(n):
                    there = cols(n * TILE, TILE)
                    Y[c, here, there] = jnp.dot(
                        U[c, here, :], w_in[:, there], preferred_element_type=F32
                    ).astype(BF16)

            for g in range(groups):
                for b in range(spans):
                    at = g * chunk + b * SPAN
                    S[c, g, b, :, 0:SPAN] = nt_dot(w_step[...], U[c, at : at + SPAN, :])
            for k in in_line:
                side_out(c, k).start()
                proj_out(c, k).start()

        def scan_span(c, b):
            at = b * SPAN
            proj = Y[c, rows(group * chunk + at, SPAN), :].astype(F32)
            pre = S[c, group, b]
            for k in in_line:
                proj = proj + YR[c, k - 1, at : at + SPAN, :].astype(F32)
                pre = pre + SR[c, k - 1, b]
            proj = proj.astype(BF16)
            step = pre + step_bias[...]
            step = jnp.maximum(step, 0.0) + jnp.log1p(jnp.exp(-jnp.abs(step)))
            decay = -jnp.exp(a_log[...]) * step
            reset = rst[c * spans + b]
            to_rows, dup = consts[0], consts[1]
            to_cols, eye = consts[2][:SPAN], consts[3][:SPAN]
            hp = lax.Precision.HIGHEST
            cum_row, step_row, seg_row = (
                exact_dot(decay, to_rows), exact_dot(step, dup), exact_dot(reset, to_rows)
            )
            cum, step_col, seg = (
                nt_dot(to_cols, decay, hp), nt_dot(eye, step, hp), nt_dot(to_cols, reset, hp)
            )
            l_at = lax.broadcasted_iota(jnp.int32, (SPAN, LANES), 1)
            t_at = lax.broadcasted_iota(jnp.int32, (SPAN, LANES), 0)
            low = l_at < SPAN
            inside = (seg[:, 0:1] == seg_row[0:1, :]) & (t_at >= jnp.where(low, l_at, l_at - SPAN))
            top = cum[SPAN - 1 : SPAN, :]
            last_seg = seg[SPAN - 1 : SPAN, :]
            carry = jnp.where(seg == 0.0, jnp.exp(cum), 0.0)
            tail = jnp.where(seg == last_seg, jnp.exp(top - cum), 0.0) * step_col
            hold = jnp.where(last_seg == 0.0, jnp.exp(top), 0.0)
            writes = proj[:, 2 * head_cols : 2 * head_cols + STATE]
            reads = proj[:, 2 * head_cols + STATE :]
            scores = nt_dot(reads, jnp.concatenate([writes, writes], axis=0))
            squares = jnp.zeros((SPAN, LANES), F32)
            for j in range(head_cols // LANES):
                a, z = 2 * j, 2 * j + 1
                part = slice(j * LANES, (j + 1) * LANES)

                def pair_col(v):
                    return jnp.where(low, v[:, a : a + 1], v[:, z : z + 1])

                def pair_row(v):
                    return jnp.where(low[0:1], v[a : a + 1, :], v[z : z + 1, :])

                x = proj[:, head_cols + j * LANES : head_cols + (j + 1) * LANES].astype(F32)
                gap = jnp.where(inside, pair_col(cum) - pair_row(cum_row), 0.0)
                weights = jnp.where(inside, jnp.exp(gap), 0.0) * scores * pair_row(step_row)
                both = jnp.concatenate(
                    [jnp.where(low, x, 0.0), jnp.where(low, 0.0, x)], axis=0
                ).astype(BF16)
                y = jnp.dot(weights.astype(BF16), both, preferred_element_type=F32)
                held = state[:, part]
                y = y + pair_col(carry) * jnp.dot(
                    reads, held.astype(BF16), preferred_element_type=F32
                )
                y = y + d_skip[:, part] * x
                fresh = tn_dot(writes, (pair_col(tail) * x).astype(BF16))
                keep_by = jnp.where(low[0:1], hold[:, a : a + 1], hold[:, z : z + 1])
                state[:, part] = fresh + keep_by * held
                gate = proj[:, part].astype(F32)
                gated = y * (gate * lax.logistic(gate))
                squares = squares + gated * gated
                gated_s[:, part] = gated
            mean = jnp.sum(squares, axis=1, keepdims=True) / head_cols
            normed = gated_s[...] * lax.rsqrt(mean + epsilon) * out_gain[...]
            normed_s[at : at + SPAN, :] = normed.astype(BF16)

        def mix(c):
            with jax.named_scope("y_wait"):
                for k in in_line:
                    side_out(c, k).wait_recv()
                    proj_out(c, k).wait_recv()
            with jax.named_scope("scan"):
                for b in range(spans):
                    scan_span(c, b)

            @pl.loop(0, feats // WIDE)
            def _(n):
                there = cols(n * WIDE, WIDE)
                PO[c, :, there] = jnp.dot(
                    normed_s[...], w_out[:, there], preferred_element_type=F32
                ).astype(BF16)

            for k in in_plane:
                part_out(c, k).start()

        def finish(c):
            with jax.named_scope("o_wait"):
                for k in in_plane:
                    part_out(c, k).wait_recv()

                @pl.when(first)
                def _():
                    for k in in_line:
                        kept_out(c, k, down(k)).wait_recv()

            @pl.loop(0, feats // (4 * TILE))
            def _(n):
                there = cols(n * 4 * TILE, 4 * TILE)
                added = PO[c, rows(lane * few, few), there].astype(F32)
                for k in in_plane:
                    added = added + PR[c, k - 1, :, there].astype(F32)
                ho[c, :, there] = (hin[c, :, there].astype(F32) + added).astype(BF16)

            @pl.when(jnp.logical_not(last))
            def _():
                hand_over(c).start()

            for k in in_plane:
                deliver(c, k, lane).start()
            keep(c).start()

        def normalise(c):
            with jax.named_scope("h_wait"):
                hand_over(c).wait_recv()
            wide = hin[c].astype(F32)
            scale = lax.rsqrt(jnp.mean(wide * wide, axis=-1, keepdims=True) + epsilon)
            un[c] = (wide * scale * gain[...]).astype(BF16)
            for k in in_line:
                z_out(c, k, group).start()
            U[c, rows(group * chunk + lane * few, few), :] = un[c, :, cols(group * depth, depth)]
            for k in in_plane:
                spread(c, 0, k, lane).start()

        def forward(c):
            for j in in_line:
                with jax.named_scope("z_wait"):
                    z_out(c, j, down(j)).wait_recv()
                for k in in_plane:
                    spread(c, j, k, lane).start()

        def gathered(c):
            for k in in_plane:
                with jax.named_scope("g_wait"):
                    for j in range(groups):
                        spread(c, j, k, left(k)).wait_recv()

        def when_chunk(index, where, name, step):
            @pl.when((index >= 0) & (index < chunks) & where)
            def _():
                with jax.named_scope(name):
                    step(index)

        later = jnp.logical_not(first)
        lag = jnp.where(first, 0, 1)

        def turn(i, _):
            when_chunk(i - 2 - lag, True, "mix", mix)
            when_chunk(i - 3 - lag, True, "finish", finish)
            when_chunk(i, later, "normalise", normalise)
            when_chunk(i, first, "permute", permute)
            when_chunk(i - 1, later, "gathered", gathered)
            when_chunk(i - lag, True, "project", project)
            when_chunk(i, later, "forward", forward)
            return 0

        lax.fori_loop(0, chunks + 4, turn, 0)

        def settle(c, _):
            keep(c).wait()
            for k in in_plane:
                deliver(c, k, left(k)).wait_recv()
                deliver(c, k, lane).wait_send()
                part_out(c, k).wait_send()
            for k in in_line:
                side_out(c, k).wait_send()
                proj_out(c, k).wait_send()

            @pl.when(first)
            def _():
                for k in in_line:
                    kept_out(c, k, group).wait_send()

            @pl.when(jnp.logical_not(first))
            def _():
                for k in in_line:
                    z_out(c, k, group).wait_send()
                for k in in_plane:
                    for j in range(groups):
                        spread(c, j, k, lane).wait_send()

            @pl.when(jnp.logical_not(last))
            def _():
                hand_over(c).wait_send()

            return 0

        lax.fori_loop(0, chunks, settle, 0)

        @pl.when(first)
        def _():
            for k in in_line:
                slots(k, group).wait_send()
                a2(k, group).wait_send()
                c2(k, group).wait_send()
            for k in in_plane:
                a1(k).wait_send()
                c3(k, lane).wait_send()
                for j in range(groups):
                    a3(j, k, lane).wait_send()

    vmem, dma = pltpu.VMEM, pltpu.SemaphoreType.DMA
    near, line = (width - 1,), (groups - 1,)
    scratch = [
        vmem((depth, n_cols), BF16),
        vmem((head_cols, feats), BF16),
        vmem((quarter, feats), BF16),
        vmem((total, depth), BF16),
        vmem((width, groups, 8, LANES), F32),
        vmem((groups, row_count // LANES, LANES), jnp.int32),
        vmem((flat, total), BF16),
        vmem((flat, LANES), F32),
        vmem((chunks, flat, depth), BF16),
        vmem((chunks, flat, depth), BF16),
        vmem((chunks, flat, n_cols), BF16),
        vmem((chunks, groups - 1, chunk, n_cols), BF16),
        vmem((chunks, groups, spans, 8, LANES), F32),
        vmem((chunks, groups - 1, spans, 8, LANES), F32),
        vmem((chunks, chunk, feats), BF16),
        vmem((chunks, width - 1, few, feats), BF16),
        vmem((chunks, few, feats), BF16),
        vmem((chunks, few, feats), BF16),
        vmem((chunks, few, feats), BF16),
        vmem((STATE, head_cols), F32),
        vmem((4, LANES, LANES), F32),
        vmem((SPAN, head_cols), F32),
        vmem((chunk, head_cols), BF16),
        dma((2,)), dma((2,)), dma((chunks,)),
    ]
    for shape in [
        near, line, line, line, (groups,) + near, near,
        (chunks,) + line, (chunks,) + line, (chunks,) + line, (chunks,) + near,
        (chunks,), (chunks,) + near, (chunks,) + line, (chunks, groups) + near,
    ]:
        scratch += [dma(shape), dma(shape)]
    anywhere = pl.BlockSpec(memory_space=pl.ANY)
    held = pl.BlockSpec(memory_space=pltpu.VMEM)
    return pl.pallas_call(
        kernel,
        out_shape=jax.ShapeDtypeStruct((row_count, feat_local), BF16),
        in_specs=[
            anywhere, held, held, held, anywhere, held, held, held, held, held, anywhere
        ],
        out_specs=anywhere,
        scratch_shapes=scratch,
        compiler_params=pltpu.CompilerParams(
            collective_id=0, has_side_effects=True, vmem_limit_bytes=63 * 1024 * 1024
        ),
    )(tokens, dest_slot, resets, gain, w_in, w_step, step_bias, a_log, d_skip, out_gain, w_out)


def per_device(
    tokens, dest_slot, doc_reset, norm_gain, w_in, w_step, step_bias, a_log, d_skip, out_gain, w_out
):
    group = lax.axis_index("dp")
    row_count = tokens.shape[0]
    depth = w_in.shape[1]
    own_step = lax.dynamic_slice_in_dim(w_step[0], group * depth, depth, axis=0).T
    resets = doc_reset.astype(F32).reshape(-1, 1, SPAN)
    resets = jnp.broadcast_to(jnp.pad(resets, ((0, 0), (0, 0), (0, LANES - SPAN))),
                              (row_count // SPAN, 8, LANES))
    out = relay(
        tokens,
        dest_slot.reshape(-1, LANES),
        resets,
        norm_gain,
        w_in[0],
        own_step,
        step_bias.reshape(-1, 1),
        a_log.reshape(-1, 1),
        jnp.repeat(d_skip, HEAD_DIM, axis=1),
        out_gain,
        w_out[0],
    )
    return out[None]


def solution(mesh):
    placed = (
        P("dp", "tensor"),
        P("dp"),
        P("dp"),
        P("section", None),
        P("section", "dp", "tensor"),
        P("section", None, "tensor"),
        P("section", "tensor"),
        P("section", "tensor"),
        P("section", "tensor"),
        P("section", "tensor"),
        P("section", "tensor", None),
    )
    return jax.shard_map(
        per_device,
        mesh=mesh,
        in_specs=placed,
        out_specs=P("section", "dp", "tensor"),
        check_vma=False,
    )
```
